128 devices in a mesh: seq: 32 (over x, z, y_lo), head: 4 (over y_hi, core).
Axes of the slice: x: 4, y: 4 (y_hi: 2, y_lo: 2; y = y_hi * 2 + y_lo), z: 4, core: 2. Of those that a mesh axis runs over, the one named last changes fastest.
Arguments:
- q_self: bfloat16 [16384, 4096], P('seq', 'head'), may hold values from -9 to 9
- k_self: bfloat16 [16384, 4096], P('seq', 'head'), may hold values from -9 to 9
- v_self: bfloat16 [16384, 4096], P('seq', 'head'), may hold values from -6 to 6
- doc_ids: int32 [16384], P('seq'), may hold values from 0 to 7, never falling along the last dimension, each value on 1 to 4096 neighbouring positions
- q_cross: bfloat16 [16384, 4096], P('seq', 'head'), may hold values from -40 to 40
- latents: bfloat16 [1024, 1280], P(('seq', 'head')), may hold values from -6 to 6
- w_latent: bfloat16 [1280, 2, 4096], P(None, None, 'head'), may hold values from -0.15625 to 0.15625
- visibility: int32 [16, 128], P(None, 'seq'), may hold values from 0 to 1, as said below
- cross_gate: float32 [4096], P('head'), may hold values from -1.5 to 1.5
Outputs:
- cross_mixed: bfloat16 [16384, 4096], P('seq', 'head')
- self_mixed: bfloat16 [16384, 4096], P('seq', 'head')
The draws below stay inside these ranges and needn't reach their ends.
Inputs may be any that keep to these rules, and one draw needn't show every extreme that they name: `doc_ids`: ids never fall along the tokens; each document holds 1 to 4096 tokens and one holds exactly 4096. `visibility`: 1 where the text tile may attend to the image, else 0; some text tiles see no image.
All inputs are finite; a program needn't handle non-finite values.
Results may differ from the reference program's by a relative error of at most 0.012.
The reference program's roundings to bfloat16 on the way count: a program that leaves them out, or rounds other values in their place, can miss the bound.
Values may be sent and summed in bfloat16 or wider, within the bound.
No kernel may reach another device: no remote copies, remote signals or barrier semaphores. Data moves between devices by JAX's collectives and lax.ppermute only.
A program may use at most 192 MiB of HBM per device.

```python
import math
import jax
import jax.numpy as jnp
import numpy as np
from jax import lax

HEADS = 32
HD = 128
VIS = 1280
LAT = 64
IMAGES = 16
TILE = 128
DOCS = 8
TOK_DEV = 512
TOKENS = 16384
TBLOCKS = 128
DOC_MOST = 4096


def self_pair(key):
    base_key = jax.random.fold_in(key, 101)
    query_key, keys_key = jax.random.split(base_key, 2)
    full_shape = (TOKENS, HEADS * HD)
    queries = jax.random.truncated_normal(query_key, -6.0, 6.0, full_shape, jnp.float32)
    keys_drawn = jax.random.truncated_normal(keys_key, -6.0, 6.0, full_shape, jnp.float32)
    return (queries, keys_drawn)


def draw_q_self(key, part):
    return self_pair(key)[0].astype(jnp.bfloat16)


def draw_k_self(key, part):
    return self_pair(key)[1].astype(jnp.bfloat16)


def draw_q_cross(key, part):
    base_key = jax.random.fold_in(key, 303)
    value_key = jax.random.fold_in(base_key, 0)
    full_shape = (TOKENS, HEADS * HD)
    queries = jax.random.truncated_normal(value_key, -6.0, 6.0, full_shape, jnp.float32)
    return queries.astype(jnp.bfloat16)


def draw_visibility(key, part):
    base_key = jax.random.fold_in(key, 505)
    bits_key, lead_key, inner_key = jax.random.split(base_key, 3)
    drawn = jax.random.randint(bits_key, (IMAGES, TBLOCKS), 0, 2, dtype=jnp.int32)
    leading = jax.random.randint(lead_key, (), 1, 4, dtype=jnp.int32)
    inner_tile = jax.random.randint(inner_key, (), 4, TBLOCKS - 1, dtype=jnp.int32)
    tile_index = jnp.arange(TBLOCKS, dtype=jnp.int32)
    image_index = jnp.arange(IMAGES, dtype=jnp.int32)
    blank = (tile_index < leading) | (tile_index == inner_tile)
    drawn = jnp.where(blank[None, :], 0, drawn)
    corner = (image_index[:, None] == 0) & (tile_index[None, :] == TBLOCKS - 1)
    drawn = jnp.where(corner, 1, drawn)
    return drawn.astype(jnp.int32)


def level_of(key, shape, pieces, smallest, top_value):
    gain = 1.0
    for position, blocks in pieces:
        heights = jax.random.uniform(jax.random.fold_in(jax.random.fold_in(key, 6), position), (blocks,), jnp.float32, smallest / len(pieces), top_value / len(pieces))
        gain = gain * jnp.repeat(jnp.exp(heights), shape[position] // blocks).reshape((-1,) + (1,) * (len(shape) - 1 - position))
    return gain


def length_profile(amount, total, bound, slope):
    weights = [(1 << 20) // math.isqrt(standing ** slope) + 1 for standing in range(2, amount + 1)]
    spare, given = total - bound - (amount - 1), [1] * (amount - 1)
    while spare > 0:
        movable = [i for i in range(amount - 1) if given[i] < bound]
        whole, left = sum([weights[i] for i in movable]), spare
        for i in movable:
            addition = min(bound - given[i], max(1, left * weights[i] // whole), spare)
            given[i] = given[i] + addition
            spare = spare - addition
    return np.array([bound] + given)


def ragged_sizes(own_key, count, total, reach, lean):
    if count == 2:
        one = jax.random.randint(own_key, (), max(1, total - reach), min(reach, total - 1) + 1)
        return jnp.stack([one, total - one])
    sizes = jnp.asarray(length_profile(count, total, reach, lean), jnp.int32)
    twos = (count - 1) // 2
    giver, receiver = sizes[1:1 + 2 * twos:2], sizes[2:2 + 2 * twos:2]
    slack = jnp.minimum(giver - 1, reach - receiver)
    passed = jax.random.randint(jax.random.fold_in(own_key, 1), (twos,), 0, 1 << 20) % (slack + 1)
    sizes = sizes.at[1:1 + 2 * twos:2].set(giver - passed).at[2:2 + 2 * twos:2].set(receiver + passed)
    return sizes[jax.random.permutation(jax.random.fold_in(own_key, 2), count)]


def noise(stream_key, extent, deviation, reach, cuts=(), held_as=jnp.bfloat16):
    entries = jax.random.normal(stream_key, extent, jnp.float32) * deviation
    if len(cuts) > 0:
        entries = level_of(stream_key, extent, cuts, -0.22, 0.18) * entries
    return jnp.clip(entries, min=-reach, max=reach).astype(held_as)


def setup_inputs(seed: int = 0) -> dict:
    key_list = jax.random.split(jax.random.key(seed), 10)
    q_self = draw_q_self(jax.random.fold_in(key_list[9], 71), 0)
    k_self = draw_k_self(jax.random.fold_in(key_list[9], 71), 0)
    v_self = noise(key_list[2], (TOKENS, HEADS * HD), 1.0, 6.0, ((0, 32), (1, 4)))
    doc_ids = jnp.searchsorted(jnp.cumsum(ragged_sizes(key_list[3], DOCS, TOKENS, DOC_MOST, 1)), jnp.arange(TOKENS), side="right").astype(jnp.int32)
    q_cross = draw_q_cross(jax.random.fold_in(key_list[9], 71), 0)
    latents = noise(key_list[5], (IMAGES * LAT, VIS), 1.0, 6.0, ((0, 128),))
    w_latent = noise(key_list[6], (VIS, 2, HEADS * HD), VIS ** -0.5, 0.15625, ((2, 4),))
    visibility = draw_visibility(jax.random.fold_in(key_list[9], 71), 0)
    cross_gate = jnp.clip(jax.random.uniform(key_list[8], (HEADS * HD,), jnp.float32, -1.5, 1.5) * level_of(key_list[8], (HEADS * HD,), ((0, 4),), -0.4, 0.0), -1.5, 1.5)
    return {"q_self": q_self, "k_self": k_self, "v_self": v_self, "doc_ids": doc_ids, "q_cross": q_cross, "latents": latents, "w_latent": w_latent, "visibility": visibility, "cross_gate": cross_gate}


NEG_LARGE = -1e+30

def reference(q_self, k_self, v_self, doc_ids, q_cross, latents, w_latent, visibility, cross_gate):
    width = HEADS * HD
    score_scale = 1.0 / math.sqrt(HD)
    latent_kv = jnp.dot(latents, w_latent.reshape(VIS, 2 * width), preferred_element_type=jnp.float32).astype(jnp.bfloat16)
    key_latent = latent_kv[:, :width].reshape(IMAGES * LAT, HEADS, HD).transpose(1, 0, 2)
    value_latent = latent_kv[:, width:].reshape(IMAGES * LAT, HEADS, HD).transpose(1, 0, 2)
    query_cross = q_cross.reshape(TOKENS, HEADS, HD).transpose(1, 0, 2)
    visible_cross = jnp.repeat(jnp.repeat(visibility.T == 1, TILE, axis=0), LAT, axis=1)
    has_image = jnp.any(visible_cross, axis=1, keepdims=True)

    def cross_head(operands):
        query_rows, key_rows, value_rows = operands
        scores = jnp.dot(query_rows, key_rows.T, preferred_element_type=jnp.float32) * score_scale
        scores = jnp.where(visible_cross, scores, NEG_LARGE)
        row_top = lax.optimization_barrier(jnp.max(scores, axis=1, keepdims=True))
        weights = jnp.where(visible_cross, jnp.exp(scores - row_top), 0.0)
        row_total = lax.optimization_barrier(jnp.sum(weights, axis=1, keepdims=True))
        summed = jnp.dot(weights.astype(jnp.bfloat16), value_rows, preferred_element_type=jnp.float32)
        divisor = row_total + (1.0 - has_image.astype(row_total.dtype))
        return jnp.where(has_image, summed / divisor, 0.0)
    cross_out = lax.map(cross_head, (query_cross, key_latent, value_latent))
    cross_mixed = (cross_out.transpose(1, 0, 2).reshape(TOKENS, width) * jnp.tanh(cross_gate)[None, :]).astype(jnp.bfloat16)
    block_count = TOKENS // TOK_DEV
    window = min(TOKENS, DOC_MOST + TOK_DEV)
    query_self = q_self.reshape(TOKENS, HEADS, HD).transpose(1, 0, 2)
    key_self = k_self.reshape(TOKENS, HEADS, HD).transpose(1, 0, 2)
    value_self = v_self.reshape(TOKENS, HEADS, HD).transpose(1, 0, 2)
    block_starts = jnp.arange(block_count, dtype=jnp.int32) * TOK_DEV

    def self_head(operands):
        query_rows, key_rows, value_rows = operands

        def self_block(block):
            query_block, block_start, query_docs = block
            key_start = jnp.clip(block_start + TOK_DEV - window, 0, TOKENS - window).astype(jnp.int32)
            key_block = lax.dynamic_slice_in_dim(key_rows, key_start, window, 0)
            value_block = lax.dynamic_slice_in_dim(value_rows, key_start, window, 0)
            key_docs = lax.dynamic_slice_in_dim(doc_ids, key_start, window, 0)
            key_pos = key_start + jnp.arange(window, dtype=jnp.int32)
            query_pos = block_start + jnp.arange(TOK_DEV, dtype=jnp.int32)
            scores = jnp.dot(query_block, key_block.T, preferred_element_type=jnp.float32) * score_scale
            visible = (key_docs[None, :] == query_docs[:, None]) & (key_pos[None, :] <= query_pos[:, None])
            scores = jnp.where(visible, scores, NEG_LARGE)
            row_top = lax.optimization_barrier(jnp.max(scores, axis=1, keepdims=True))
            weights = jnp.where(visible, jnp.exp(scores - row_top), 0.0)
            row_total = lax.optimization_barrier(jnp.sum(weights, axis=1, keepdims=True))
            summed = jnp.dot(weights.astype(jnp.bfloat16), value_block, preferred_element_type=jnp.float32)
            return summed / row_total
        blocks = (query_rows.reshape(block_count, TOK_DEV, HD), block_starts, doc_ids.reshape(block_count, TOK_DEV))
        return lax.map(self_block, blocks).reshape(TOKENS, HD)
    self_out = lax.map(self_head, (query_self, key_self, value_self))
    self_mixed = self_out.transpose(1, 0, 2).reshape(TOKENS, width).astype(jnp.bfloat16)
    return (cross_mixed, self_mixed)
```

```python
import functools
import math

import jax
import jax.numpy as jnp
from jax import lax
from jax.experimental import pallas as pl
from jax.experimental.pallas import tpu as pltpu
from jax.sharding import PartitionSpec as P

HD = 128
LAT = 64
TILE = 128
NEG_LARGE = -1e30
EXP2_SCALE = math.log2(math.e) / math.sqrt(HD)

NX, NZ, NYL, NYH, NCORE = 4, 4, 2, 2, 2
GROUP = NZ * NYL
BOTH = ("seq", "head")


def device_pairs(move):
    pairs = []
    for x in range(NX):
        for z in range(NZ):
            for y in range(NYL * NYH):
                for core in range(NCORE):
                    there = move(x, z, y, core)
                    pairs.append(tuple(
                        ((a * NZ + b) * NYL + c % NYL) * (NYH * NCORE) + (c // NYL) * NCORE + d
                        for a, b, c, d in ((x, z, y, core), there)
                    ))
    return pairs


def hop(value, move):
    return lax.ppermute(value, BOTH, device_pairs(move))


def rotated(place, turn, sign):
    z, y = place // NYL, place % NYL
    z = (z + sign * (turn // NYL) + NZ) % NZ
    y = (y + turn) % NYL
    return z * NYL + y


def turn_hop(value, turn):
    dz, dy = turn // NYL, turn % NYL
    return hop(
        value,
        lambda x, z, y, c: (x, (z + dz) % NZ, (y // NYL) * NYL + (y + dy) % NYL, c),
    )


def split_kernel(place_ref, q_ref, k_ref, v_ref, *rest):
    kv_out, q_out = rest[:GROUP], rest[GROUP : 2 * GROUP]
    q_buf, k_buf, v_buf, in_sems, out_sems = rest[2 * GROUP :]
    loads = []
    for n, (source, buf) in enumerate(((k_ref, k_buf), (v_ref, v_buf), (q_ref, q_buf))):
        copy = pltpu.make_async_copy(source, buf, in_sems.at[n])
        copy.start()
        loads.append(copy)
    copies = []
    for n, buf in enumerate((k_buf, v_buf, q_buf)):
        loads[n].wait()
        for turn in range(GROUP):
            columns = pl.ds(pl.multiple_of(place_ref[turn] * HD, HD), HD)
            target = q_out[turn] if n == 2 else kv_out[turn].at[n]
            copy = pltpu.make_async_copy(buf.at[:, columns], target, out_sems.at[turn * 3 + n])
            copy.start()
            copies.append(copy)
    for copy in copies:
        copy.wait()


def split_heads(targets, q, k, v):
    rows = q.shape[0]
    anywhere = pl.BlockSpec(memory_space=pl.ANY)
    out = pl.pallas_call(
        split_kernel,
        grid_spec=pltpu.PrefetchScalarGridSpec(
            num_scalar_prefetch=1,
            grid=(1,),
            in_specs=[anywhere] * 3,
            out_specs=[anywhere] * (2 * GROUP),
            scratch_shapes=[pltpu.VMEM(q.shape, q.dtype)] * 3
            + [pltpu.SemaphoreType.DMA((3,)), pltpu.SemaphoreType.DMA((3 * GROUP,))],
        ),
        out_shape=[jax.ShapeDtypeStruct((2, rows, HD), q.dtype)] * GROUP
        + [jax.ShapeDtypeStruct((rows, HD), q.dtype)] * GROUP,
        name="split_heads",
    )(targets, q, k, v)
    return out[:GROUP], out[GROUP:]


def join_kernel(source_ref, *rest):
    pieces, out, buf, sems, out_sem = rest[:GROUP], *rest[GROUP:]
    copies = []
    for turn in range(GROUP):
        columns = pl.ds(pl.multiple_of(source_ref[turn] * HD, HD), HD)
        copy = pltpu.make_async_copy(pieces[turn], buf.at[:, columns], sems.at[turn])
        copy.start()
        copies.append(copy)
    for copy in copies:
        copy.wait()
    copy = pltpu.make_async_copy(buf, out, out_sem)
    copy.start()
    copy.wait()


def join_heads(sources, pieces):
    rows = pieces[0].shape[0]
    anywhere = pl.BlockSpec(memory_space=pl.ANY)
    return pl.pallas_call(
        join_kernel,
        grid_spec=pltpu.PrefetchScalarGridSpec(
            num_scalar_prefetch=1,
            grid=(1,),
            in_specs=[anywhere] * GROUP,
            out_specs=anywhere,
            scratch_shapes=[
                pltpu.VMEM((rows, GROUP * HD), pieces[0].dtype),
                pltpu.SemaphoreType.DMA((GROUP,)),
                pltpu.SemaphoreType.DMA,
            ],
        ),
        out_shape=jax.ShapeDtypeStruct((rows, GROUP * HD), pieces[0].dtype),
        name="join_heads",
    )(sources, *pieces)


def self_kernel(rows, begins_ref, place_ref, *rest):
    own_kv, past_kv, own_q = (rest[n * GROUP : (n + 1) * GROUP] for n in range(3))
    outs = rest[3 * GROUP : 4 * GROUP]
    kbuf, vbuf, qbuf, obuf, top, total, accum, in_sems, out_sems = rest[4 * GROUP :]
    span = GROUP * rows
    copies = []
    for turn in range(GROUP):
        slot = place_ref[GROUP + turn] * rows
        moves = []
        for n, (pieces, base) in enumerate(((past_kv, 0), (own_kv, span))):
            to = pl.ds(pl.multiple_of(base + slot, rows), rows)
            moves += [(pieces[turn].at[0], kbuf.at[to]), (pieces[turn].at[1], vbuf.at[to])]
        moves.append((own_q[turn], qbuf.at[pl.ds(pl.multiple_of(slot, rows), rows)]))
        for n, (source, target) in enumerate(moves):
            copy = pltpu.make_async_copy(source, target, in_sems.at[turn * 5 + n])
            copy.start()
            copies.append(copy)
    for copy in copies:
        copy.wait()

    def begin_of(position):
        found = begins_ref[0]
        for d in range(1, 8):
            found = jnp.where(begins_ref[d] <= position, begins_ref[d], found)
        return found

    row_in = lax.broadcasted_iota(jnp.int32, (rows, 1), 0)
    col_in = lax.broadcasted_iota(jnp.int32, (rows, rows), 1)

    def chunk(c, carried):
        first = span + c * rows
        row = first + row_in
        row_begin = jnp.full((rows, 1), begins_ref[0], jnp.int32)
        for d in range(1, 8):
            row_begin = jnp.where(begins_ref[d] <= row, begins_ref[d], row_begin)
        begin_low = jnp.maximum(begin_of(first), 0)
        begin_high = begin_of(first + rows - 1)
        q = qbuf[pl.ds(pl.multiple_of(c * rows, rows), rows), :]

        def scores_of(block):
            keys = kbuf[pl.ds(pl.multiple_of(block * rows, rows), rows), :]
            return lax.dot_general(
                q, keys, (((1,), (1,)), ((), ())), preferred_element_type=jnp.float32
            )

        def absorb(block, masked, opening):
            values = vbuf[pl.ds(pl.multiple_of(block * rows, rows), rows), :]
            scores = scores_of(block)
            if masked:
                col = block * rows + col_in
                scores = jnp.where((col >= row_begin) & (col <= row), scores, NEG_LARGE)
            block_top = jnp.max(scores, axis=1, keepdims=True)
            if opening:
                new_top = jnp.broadcast_to(block_top, (rows, HD))
            else:
                old_top = top[...]
                new_top = jnp.maximum(old_top, block_top)
            parts = [
                jnp.exp2((scores[:, n * HD : (n + 1) * HD] - new_top) * EXP2_SCALE)
                for n in range(rows // HD)
            ]
            lane_total = functools.reduce(jnp.add, parts)
            weights = jnp.concatenate([part.astype(jnp.bfloat16) for part in parts], axis=1)
            mixed = jnp.dot(weights, values, preferred_element_type=jnp.float32)
            if opening:
                total[...] = lane_total
                accum[...] = mixed
            else:
                factor = jnp.exp2((old_top - new_top) * EXP2_SCALE)
                total[...] = total[...] * factor + lane_total
                accum[...] = accum[...] * factor + mixed
            top[...] = new_top

        diagonal = first // rows
        absorb(diagonal, True, True)
        low_block = begin_low // rows
        clear_block = jnp.clip((begin_high + rows - 1) // rows, low_block, diagonal)

        def edge(block, carried):
            absorb(block, True, False)
            return carried

        def inner(block, carried):
            absorb(block, False, False)
            return carried

        lax.fori_loop(low_block, clear_block, edge, 0)
        lax.fori_loop(clear_block, diagonal, inner, 0)
        whole = jnp.sum(total[...], axis=1, keepdims=True)
        obuf[pl.ds(pl.multiple_of(c * rows, rows), rows), :] = (accum[...] / whole).astype(
            jnp.bfloat16
        )
        return carried

    lax.fori_loop(0, GROUP, chunk, 0)
    copies = []
    for turn in range(GROUP):
        at = pl.ds(pl.multiple_of(place_ref[turn] * rows, rows), rows)
        copy = pltpu.make_async_copy(obuf.at[at], outs[turn], out_sems.at[turn])
        copy.start()
        copies.append(copy)
    for copy in copies:
        copy.wait()


def self_attention(begins, places, own_kv, past_kv, own_q):
    rows = own_q[0].shape[0]
    span = rows * GROUP
    anywhere = pl.BlockSpec(memory_space=pl.ANY)
    return pl.pallas_call(
        functools.partial(self_kernel, rows),
        grid_spec=pltpu.PrefetchScalarGridSpec(
            num_scalar_prefetch=2,
            grid=(1,),
            in_specs=[anywhere] * (3 * GROUP),
            out_specs=[anywhere] * GROUP,
            scratch_shapes=[
                pltpu.VMEM((2 * span, HD), jnp.bfloat16),
                pltpu.VMEM((2 * span, HD), jnp.bfloat16),
                pltpu.VMEM((span, HD), jnp.bfloat16),
                pltpu.VMEM((span, HD), jnp.bfloat16),
                pltpu.VMEM((rows, HD), jnp.float32),
                pltpu.VMEM((rows, HD), jnp.float32),
                pltpu.VMEM((rows, HD), jnp.float32),
                pltpu.SemaphoreType.DMA((5 * GROUP,)),
                pltpu.SemaphoreType.DMA((GROUP,)),
            ],
        ),
        out_shape=[jax.ShapeDtypeStruct((rows, HD), jnp.bfloat16)] * GROUP,
        name="self_attention",
    )(begins, places, *own_kv, *past_kv, *own_q)


def cross_kernel(
    rows, width, seen_ref, q_ref, lat_a, lat_b, wk_ref, wv_ref, mask_ref, gate_ref, out_ref,
    keys, values,
):
    heads = wk_ref.shape[1] // HD
    half = lat_a.shape[0]
    for n, lat in enumerate((lat_a, lat_b)):
        part = lat[:, :width]
        at = pl.ds(n * half, half)
        keys[at, :] = jnp.dot(
            part, wk_ref[...], preferred_element_type=jnp.float32
        ).astype(jnp.bfloat16)
        values[at, :] = jnp.dot(
            part, wv_ref[...], preferred_element_type=jnp.float32
        ).astype(jnp.bfloat16)
    for tile in range(rows // TILE):
        visible = mask_ref[tile : tile + 1, :] > 0
        seen = jnp.full((TILE, HD), seen_ref[tile], jnp.int32) > 0
        for head in range(heads):
            mine = slice(head * HD, (head + 1) * HD)
            scores = lax.dot_general(
                q_ref[tile * TILE : (tile + 1) * TILE, mine],
                keys[:, mine],
                (((1,), (1,)), ((), ())),
                preferred_element_type=jnp.float32,
            )
            scores = jnp.where(visible, scores, NEG_LARGE)
            row_top = jnp.max(scores, axis=1, keepdims=True)
            weights = jnp.exp2((scores - row_top) * EXP2_SCALE)
            row_total = jnp.sum(weights, axis=1, keepdims=True)
            mixed = jnp.dot(
                weights.astype(jnp.bfloat16), values[:, mine], preferred_element_type=jnp.float32
            )
            mixed = jnp.where(seen, mixed / row_total, 0.0) * gate_ref[:1, mine]
            out_ref[tile * TILE : (tile + 1) * TILE, mine] = mixed.astype(jnp.bfloat16)


def cross_attention(seen, q, lat_a, lat_b, w_flat, mask, gate):
    rows, columns = q.shape
    width = w_flat.shape[0]
    step = 2 * HD
    steps = columns // step
    count = lat_a.shape[0] + lat_b.shape[0]
    return pl.pallas_call(
        functools.partial(cross_kernel, rows, width),
        grid_spec=pltpu.PrefetchScalarGridSpec(
            num_scalar_prefetch=1,
            grid=(steps,),
            in_specs=[
                pl.BlockSpec((rows, step), lambda i, s: (0, i)),
                pl.BlockSpec(lat_a.shape, lambda i, s: (0, 0)),
                pl.BlockSpec(lat_b.shape, lambda i, s: (0, 0)),
                pl.BlockSpec((width, step), lambda i, s: (0, i)),
                pl.BlockSpec((width, step), lambda i, s: (0, i + steps)),
                pl.BlockSpec(mask.shape, lambda i, s: (0, 0)),
                pl.BlockSpec((8, step), lambda i, s: (0, i)),
            ],
            out_specs=pl.BlockSpec((rows, step), lambda i, s: (0, i)),
            scratch_shapes=[pltpu.VMEM((count, step), jnp.bfloat16)] * 2,
        ),
        out_shape=jax.ShapeDtypeStruct((rows, columns), jnp.bfloat16),
        name="cross_attention",
    )(seen, q, lat_a, lat_b, w_flat, w_flat, mask, gate)


def body(q_self, k_self, v_self, doc_ids, q_cross, latents, w_latent, visibility, cross_gate):
    rows, columns = q_self.shape
    width = latents.shape[1]
    position = lax.axis_index("seq")
    plane = position // GROUP
    place = position % GROUP
    z_here = place // NYL
    turns = jnp.arange(GROUP, dtype=jnp.int32)
    targets = rotated(place, turns, 1)
    sources = rotated(place, turns, -1)
    places = jnp.concatenate([targets, sources]).astype(jnp.int32)

    below = jnp.sum(
        (doc_ids[None, :] < jnp.arange(8, dtype=jnp.int32)[:, None]).astype(jnp.int32), axis=1
    )
    lane = jnp.arange(HD, dtype=jnp.int32)[None, :]
    digits = jnp.where(lane == 0, (below // 16)[:, None], 0) + jnp.where(
        lane == 1, (below % 16)[:, None], 0
    )
    lat = jnp.concatenate([latents, digits.astype(jnp.bfloat16)], axis=1)
    kv_pieces, q_pieces = split_heads(places, q_self, k_self, v_self)
    lat, kept = lax.optimization_barrier((lat, kv_pieces[0]))
    lat = jnp.concatenate(
        [lat] + [hop(lat, lambda x, z, y, c, d=d: (x, z, (y + d) % 4, c)) for d in (1, 2, 3)]
    )
    lat = jnp.concatenate(
        [lat] + [hop(lat, lambda x, z, y, c, d=d: (x, (z + d) % 4, y, c)) for d in (1, 2, 3)]
    )
    lat_a = jnp.concatenate(
        [lat] + [hop(lat, lambda x, z, y, c, d=d: ((x + d) % 4, z, y, c)) for d in (1, 2, 3)]
    )
    lat_b = hop(lat_a, lambda x, z, y, c: (x, z, y, 1 - c))

    counted = sum(
        jnp.sum(part[:, width : width + 2].astype(jnp.float32).reshape(-1, 8, 2), axis=0)
        for part in (lat_a, lat_b)
    ).astype(jnp.int32) // (NYH * NCORE)
    begins = counted[:, 0] * 16 + counted[:, 1] - (plane - 1) * GROUP * rows

    own_kv = [kv_pieces[0]] + [turn_hop(kv_pieces[t], t) for t in range(1, GROUP)]
    past_kv = [
        hop(piece, lambda x, z, y, c: ((x + 1) % 4, z, y, c)) for piece in own_kv
    ]
    own_q = [q_pieces[0]] + [turn_hop(q_pieces[t], t) for t in range(1, GROUP)]
    mixed = self_attention(begins, places, own_kv, past_kv, own_q)
    back = [mixed[0]] + [turn_hop(mixed[t], t) for t in range(1, GROUP)]
    self_mixed = join_heads(sources.astype(jnp.int32), back)

    away = jnp.arange(16, dtype=jnp.int32)
    image = ((plane - away // NZ + NX) % NX) * NZ + (z_here - away % NZ + NZ) % NZ
    chosen = jnp.take(visibility, image, axis=0)
    mask = jnp.tile(jnp.repeat((chosen.T == 1).astype(jnp.float32), LAT // 2, axis=1), (2, 2))
    seen = jnp.any(visibility == 1, axis=0).astype(jnp.int32)
    w_flat = w_latent.reshape(width, 2 * columns)
    gate = jnp.broadcast_to(jnp.tanh(cross_gate)[None, :], (8, columns))
    cross_mixed = cross_attention(seen, q_cross, lat_a, lat_b, w_flat, mask, gate)
    return (cross_mixed, self_mixed)


def solution(mesh):
    placed = (
        P("seq", "head"),
        P("seq", "head"),
        P("seq", "head"),
        P("seq"),
        P("seq", "head"),
        P(("seq", "head"), None),
        P(None, None, "head"),
        P(None, "seq"),
        P("head"),
    )
    return jax.shard_map(
        body,
        mesh=mesh,
        in_specs=placed,
        out_specs=(P("seq", "head"), P("seq", "head")),
        check_vma=False,
    )
```

```python
import functools
import math

import jax
import jax.numpy as jnp
from jax import lax
from jax.experimental import pallas as pl
from jax.experimental.pallas import tpu as pltpu
from jax.sharding import PartitionSpec as P


HD = 128
LAT = 64
TILE = 128
NEG_LARGE = -1e30
EXP2_SCALE = math.log2(math.e) / math.sqrt(HD)

NX, NZ, NYL, NYH, NCORE = 4, 4, 2, 2, 2
GROUP = NZ * NYL
BOTH = ("seq", "head")
CROSS_FIRST = 2
RELAYOUT_AT = 0
QKV_ORDER = (1, 2, 4, 6, 3, 5, 7)


def device_pairs(move):
    pairs = []
    for x in range(NX):
        for z in range(NZ):
            for y in range(NYL * NYH):
                for core in range(NCORE):
                    there = move(x, z, y, core)
                    pairs.append(tuple(
                        ((a * NZ + b) * NYL + c % NYL) * (NYH * NCORE) + (c // NYL) * NCORE + d
                        for a, b, c, d in ((x, z, y, core), there)
                    ))
    return pairs


def hop(value, move):
    return lax.ppermute(value, BOTH, device_pairs(move))


def rotated(place, turn, sign):
    z, y = place // NYL, place % NYL
    z = (z + sign * (turn // NYL) + NZ) % NZ
    y = (y + turn) % NYL
    return z * NYL + y


def turn_hop(value, turn):
    dz, dy = turn // NYL, turn % NYL
    return hop(value, lambda x, z, y, c: (x, (z + dz) % NZ, (y // NYL) * NYL + (y + dy) % NYL, c))


def split_kernel(place_ref, q_ref, k_ref, v_ref, *rest):
    outs = rest[:GROUP]
    q_buf, k_buf, v_buf, in_sems, out_sems = rest[GROUP:]
    loads = []
    for n, (source, buf) in enumerate(((k_ref, k_buf), (v_ref, v_buf), (q_ref, q_buf))):
        copy = pltpu.make_async_copy(source, buf, in_sems.at[n])
        copy.start()
        loads.append(copy)
    copies = []
    for n, buf in enumerate((k_buf, v_buf, q_buf)):
        loads[n].wait()
        for turn in range(GROUP):
            columns = pl.ds(pl.multiple_of(place_ref[turn] * HD, HD), HD)
            copy = pltpu.make_async_copy(
                buf.at[:, columns], outs[turn].at[n], out_sems.at[turn * 3 + n]
            )
            copy.start()
            copies.append(copy)
    for copy in copies:
        copy.wait()


def split_heads(targets, q, k, v):
    rows = q.shape[0]
    anywhere = pl.BlockSpec(memory_space=pl.ANY)
    return pl.pallas_call(
        split_kernel,
        grid_spec=pltpu.PrefetchScalarGridSpec(
            num_scalar_prefetch=1,
            grid=(1,),
            in_specs=[anywhere] * 3,
            out_specs=[anywhere] * GROUP,
            scratch_shapes=[pltpu.VMEM(q.shape, q.dtype)] * 3
            + [pltpu.SemaphoreType.DMA((3,)), pltpu.SemaphoreType.DMA((3 * GROUP,))],
        ),
        out_shape=[jax.ShapeDtypeStruct((3, rows, HD), q.dtype)] * GROUP,
        name="split_heads",
    )(targets, q, k, v)


def join_kernel(source_ref, *rest):
    pieces, out, buf, sems, out_sem = rest[:GROUP], *rest[GROUP:]
    copies = []
    for turn in range(GROUP):
        columns = pl.ds(pl.multiple_of(source_ref[turn] * HD, HD), HD)
        copy = pltpu.make_async_copy(pieces[turn], buf.at[:, columns], sems.at[turn])
        copy.start()
        copies.append(copy)
    for copy in copies:
        copy.wait()
    copy = pltpu.make_async_copy(buf, out, out_sem)
    copy.start()
    copy.wait()


def join_heads(sources, pieces):
    rows = pieces[0].shape[0]
    anywhere = pl.BlockSpec(memory_space=pl.ANY)
    return pl.pallas_call(
        join_kernel,
        grid_spec=pltpu.PrefetchScalarGridSpec(
            num_scalar_prefetch=1,
            grid=(1,),
            in_specs=[anywhere] * GROUP,
            out_specs=anywhere,
            scratch_shapes=[
                pltpu.VMEM((rows, GROUP * HD), pieces[0].dtype),
                pltpu.SemaphoreType.DMA((GROUP,)),
                pltpu.SemaphoreType.DMA,
            ],
        ),
        out_shape=jax.ShapeDtypeStruct((rows, GROUP * HD), pieces[0].dtype),
        name="join_heads",
    )(sources, *pieces)


def self_kernel(rows, begins_ref, place_ref, *rest):
    own, past_kv, outs = (rest[n * GROUP : (n + 1) * GROUP] for n in range(3))
    kbuf, vbuf, qbuf, obuf, top, total, accum, in_sems, out_sems = rest[3 * GROUP :]
    span = GROUP * rows
    copies = []
    for turn in range(GROUP):
        slot = place_ref[GROUP + turn] * rows
        moves = []
        for pieces, base in ((past_kv, 0), (own, span)):
            to = pl.ds(pl.multiple_of(base + slot, rows), rows)
            moves += [(pieces[turn].at[0], kbuf.at[to]), (pieces[turn].at[1], vbuf.at[to])]
        moves.append((own[turn].at[2], qbuf.at[pl.ds(pl.multiple_of(slot, rows), rows)]))
        for n, (source, target) in enumerate(moves):
            copy = pltpu.make_async_copy(source, target, in_sems.at[turn * 5 + n])
            copy.start()
            copies.append(copy)
    for copy in copies:
        copy.wait()

    def begin_of(position):
        found = begins_ref[0]
        for d in range(1, 8):
            found = jnp.where(begins_ref[d] <= position, begins_ref[d], found)
        return found

    row_in = lax.broadcasted_iota(jnp.int32, (rows, 1), 0)
    col_in = lax.broadcasted_iota(jnp.int32, (rows, rows), 1)

    def chunk(c, carried):
        first = span + c * rows
        row = first + row_in
        row_begin = jnp.full((rows, 1), begins_ref[0], jnp.int32)
        for d in range(1, 8):
            row_begin = jnp.where(begins_ref[d] <= row, begins_ref[d], row_begin)
        begin_low = jnp.maximum(begin_of(first), 0)
        begin_high = begin_of(first + rows - 1)
        q = qbuf[pl.ds(pl.multiple_of(c * rows, rows), rows), :]

        def scores_of(block):
            keys = kbuf[pl.ds(pl.multiple_of(block * rows, rows), rows), :]
            return lax.dot_general(
                q, keys, (((1,), (1,)), ((), ())), preferred_element_type=jnp.float32
            )

        def absorb(block, masked, opening):
            values = vbuf[pl.ds(pl.multiple_of(block * rows, rows), rows), :]
            scores = scores_of(block)
            if masked:
                col = block * rows + col_in
                scores = jnp.where((col >= row_begin) & (col <= row), scores, NEG_LARGE)
            block_top = jnp.max(scores, axis=1, keepdims=True)
            if opening:
                new_top = jnp.broadcast_to(block_top, (rows, HD))
            else:
                old_top = top[...]
                new_top = jnp.maximum(old_top, block_top)
            parts = [
                jnp.exp2((scores[:, n * HD : (n + 1) * HD] - new_top) * EXP2_SCALE)
                for n in range(rows // HD)
            ]
            lane_total = functools.reduce(jnp.add, parts)
            weights = jnp.concatenate([part.astype(jnp.bfloat16) for part in parts], axis=1)
            mixed = jnp.dot(weights, values, preferred_element_type=jnp.float32)
            if opening:
                total[...] = lane_total
                accum[...] = mixed
            else:
                factor = jnp.exp2((old_top - new_top) * EXP2_SCALE)
                total[...] = total[...] * factor + lane_total
                accum[...] = accum[...] * factor + mixed
            top[...] = new_top

        diagonal = first // rows
        absorb(diagonal, True, True)
        low_block = begin_low // rows
        clear_block = jnp.clip((begin_high + rows - 1) // rows, low_block, diagonal)

        def edge(block, carried):
            absorb(block, True, False)
            return carried

        def inner(block, carried):
            absorb(block, False, False)
            return carried

        lax.fori_loop(low_block, clear_block, edge, 0)
        lax.fori_loop(clear_block, diagonal, inner, 0)
        whole = jnp.sum(total[...], axis=1, keepdims=True)
        obuf[pl.ds(pl.multiple_of(c * rows, rows), rows), :] = (accum[...] / whole).astype(
            jnp.bfloat16
        )
        return carried

    lax.fori_loop(0, GROUP, chunk, 0)
    copies = []
    for turn in range(GROUP):
        at = pl.ds(pl.multiple_of(place_ref[turn] * rows, rows), rows)
        copy = pltpu.make_async_copy(obuf.at[at], outs[turn], out_sems.at[turn])
        copy.start()
        copies.append(copy)
    for copy in copies:
        copy.wait()


def self_attention(begins, places, own, past_kv):
    rows = own[0].shape[1]
    span = rows * GROUP
    anywhere = pl.BlockSpec(memory_space=pl.ANY)
    return pl.pallas_call(
        functools.partial(self_kernel, rows),
        grid_spec=pltpu.PrefetchScalarGridSpec(
            num_scalar_prefetch=2,
            grid=(1,),
            in_specs=[anywhere] * (2 * GROUP),
            out_specs=[anywhere] * GROUP,
            scratch_shapes=[
                pltpu.VMEM((2 * span, HD), jnp.bfloat16),
                pltpu.VMEM((2 * span, HD), jnp.bfloat16),
                pltpu.VMEM((span, HD), jnp.bfloat16),
                pltpu.VMEM((span, HD), jnp.bfloat16),
                pltpu.VMEM((rows, HD), jnp.float32),
                pltpu.VMEM((rows, HD), jnp.float32),
                pltpu.VMEM((rows, HD), jnp.float32),
                pltpu.SemaphoreType.DMA((5 * GROUP,)),
                pltpu.SemaphoreType.DMA((GROUP,)),
            ],
        ),
        out_shape=[jax.ShapeDtypeStruct((rows, HD), jnp.bfloat16)] * GROUP,
        name="self_attention",
    )(begins, places, *own, *past_kv)


def cross_kernel(
    rows, width, seen_ref, q_ref, lat_a, lat_b, wk_ref, wv_ref, mask_ref, gate_ref,
    *rest,
):
    out_ref, keys, values = rest[-3:]
    heads = wk_ref.shape[1] // HD
    half = lat_a.shape[0]
    for n, lat in enumerate((lat_a, lat_b)):
        part = lat[:, :width]
        at = pl.ds(n * half, half)
        keys[at, :] = jnp.dot(
            part, wk_ref[...], preferred_element_type=jnp.float32
        ).astype(jnp.bfloat16)
        values[at, :] = jnp.dot(
            part, wv_ref[...], preferred_element_type=jnp.float32
        ).astype(jnp.bfloat16)
    for tile in range(rows // TILE):
        visible = mask_ref[tile : tile + 1, :] > 0
        seen = jnp.full((TILE, HD), seen_ref[tile], jnp.int32) > 0
        for head in range(heads):
            mine = slice(head * HD, (head + 1) * HD)
            scores = lax.dot_general(
                q_ref[tile * TILE : (tile + 1) * TILE, mine],
                keys[:, mine],
                (((1,), (1,)), ((), ())),
                preferred_element_type=jnp.float32,
            )
            scores = jnp.where(visible, scores, NEG_LARGE)
            row_top = jnp.max(scores, axis=1, keepdims=True)
            weights = jnp.exp2((scores - row_top) * EXP2_SCALE)
            row_total = jnp.sum(weights, axis=1, keepdims=True)
            mixed = jnp.dot(
                weights.astype(jnp.bfloat16), values[:, mine], preferred_element_type=jnp.float32
            )
            mixed = jnp.where(seen, mixed / row_total, 0.0) * gate_ref[:1, mine]
            out_ref[tile * TILE : (tile + 1) * TILE, mine] = mixed.astype(jnp.bfloat16)


def cross_attention(seen, q, lat_a, lat_b, w_flat, mask, gate, begin, end, earlier=None):
    rows, columns = q.shape
    width = w_flat.shape[0]
    step = 2 * HD
    steps = columns // step
    count = lat_a.shape[0] + lat_b.shape[0]
    return pl.pallas_call(
        functools.partial(cross_kernel, rows, width),
        grid_spec=pltpu.PrefetchScalarGridSpec(
            num_scalar_prefetch=1,
            grid=(end - begin,),
            in_specs=[
                pl.BlockSpec((rows, step), lambda i, s: (0, i + begin)),
                pl.BlockSpec(lat_a.shape, lambda i, s: (0, 0)),
                pl.BlockSpec(lat_b.shape, lambda i, s: (0, 0)),
                pl.BlockSpec((width, step), lambda i, s: (0, i + begin)),
                pl.BlockSpec((width, step), lambda i, s: (0, i + begin + steps)),
                pl.BlockSpec(mask.shape, lambda i, s: (0, 0)),
                pl.BlockSpec((8, step), lambda i, s: (0, i + begin)),
            ]
            + [pl.BlockSpec(memory_space=pl.ANY)] * (earlier is not None),
            out_specs=pl.BlockSpec((rows, step), lambda i, s: (0, i + begin)),
            scratch_shapes=[pltpu.VMEM((count, step), jnp.bfloat16)] * 2,
        ),
        out_shape=jax.ShapeDtypeStruct((rows, columns), jnp.bfloat16),
        input_output_aliases={} if earlier is None else {8: 0},
        name="cross_attention",
    )(
        seen, q, lat_a, lat_b, w_flat, w_flat, mask, gate,
        *(() if earlier is None else (earlier,)),
    )


def body(q_self, k_self, v_self, doc_ids, q_cross, latents, w_latent, visibility, cross_gate):
    rows, columns = q_self.shape
    width = latents.shape[1]
    position = lax.axis_index("seq")
    plane = position // GROUP
    place = position % GROUP
    z_here = place // NYL
    turns = jnp.arange(GROUP, dtype=jnp.int32)
    targets = rotated(place, turns, 1)
    sources = rotated(place, turns, -1)
    places = jnp.concatenate([targets, sources]).astype(jnp.int32)

    below = jnp.sum(
        (doc_ids[None, :] < jnp.arange(8, dtype=jnp.int32)[:, None]).astype(jnp.int32), axis=1
    )
    lane = jnp.arange(HD, dtype=jnp.int32)[None, :]
    digits = jnp.where(lane == 0, (below // 16)[:, None], 0) + jnp.where(
        lane == 1, (below % 16)[:, None], 0
    )
    lat = jnp.concatenate([latents, digits.astype(jnp.bfloat16)], axis=1)
    pieces = split_heads(places, q_self, k_self, v_self)
    lat = jnp.concatenate(
        [lat] + [hop(lat, lambda x, z, y, c, d=d: (x, z, (y + d) % 4, c)) for d in (1, 2, 3)]
    )
    lat = jnp.concatenate(
        [lat] + [hop(lat, lambda x, z, y, c, d=d: (x, (z + d) % 4, y, c)) for d in (1, 2, 3)]
    )
    lat_a = jnp.concatenate(
        [lat] + [hop(lat, lambda x, z, y, c, d=d: ((x + d) % 4, z, y, c)) for d in (1, 2, 3)]
    )
    lat_b = hop(lat_a, lambda x, z, y, c: (x, z, y, 1 - c))

    counted = sum(
        jnp.sum(part[:, width : width + 2].astype(jnp.float32).reshape(-1, 8, 2), axis=0)
        for part in (lat_a, lat_b)
    ).astype(jnp.int32) // (NYH * NCORE)
    begins = counted[:, 0] * 16 + counted[:, 1] - (plane - 1) * GROUP * rows

    own = [pieces[0]] + [turn_hop(pieces[t], t) for t in range(1, GROUP)]
    kv = [piece[:2] for piece in own]
    later = QKV_ORDER[RELAYOUT_AT]
    w_flat, kv[later] = lax.optimization_barrier(
        (w_latent.reshape(width, 2 * columns), kv[later])
    )
    past_kv = [hop(part, lambda x, z, y, c: ((x + 1) % 4, z, y, c)) for part in kv]
    away = jnp.arange(16, dtype=jnp.int32)
    image = ((plane - away // NZ + NX) % NX) * NZ + (z_here - away % NZ + NZ) % NZ
    chosen = jnp.take(visibility, image, axis=0)
    mask = jnp.tile(jnp.repeat((chosen.T == 1).astype(jnp.float32), LAT // 2, axis=1), (2, 2))
    seen = jnp.any(visibility == 1, axis=0).astype(jnp.int32)
    gate = jnp.broadcast_to(jnp.tanh(cross_gate)[None, :], (8, columns))
    operands = (seen, q_cross, lat_a, lat_b, w_flat, mask, gate)
    cross_mixed = cross_attention(*operands, 0, CROSS_FIRST)
    begins, cross_mixed = lax.optimization_barrier((begins, cross_mixed))
    mixed = self_attention(begins, places, own, past_kv)
    back = [mixed[0]] + [turn_hop(mixed[t], t) for t in range(1, GROUP)]
    self_mixed = join_heads(sources.astype(jnp.int32), back)
    cross_mixed = cross_attention(*operands, CROSS_FIRST, columns // (2 * HD), cross_mixed)
    return (cross_mixed, self_mixed)


def solution(mesh):
    placed = (
        P("seq", "head"),
        P("seq", "head"),
        P("seq", "head"),
        P("seq"),
        P("seq", "head"),
        P(("seq", "head"), None),
        P(None, None, "head"),
        P(None, "seq"),
        P("head"),
    )
    return jax.shard_map(
        body,
        mesh=mesh,
        in_specs=placed,
        out_specs=(P("seq", "head"), P("seq", "head")),
        check_vma=False,
    )
```

```python
import functools
import math

import jax
import jax.numpy as jnp
from jax import lax
from jax.experimental import pallas as pl
from jax.experimental.pallas import tpu as pltpu
from jax.sharding import PartitionSpec as P


HD = 128
LAT = 64
TILE = 128
KEYS = 256
NEG_LARGE = -1e30
EXP2_SCALE = math.log2(math.e) / math.sqrt(HD)

NX, NZ, NYL, NYH, NCORE = 4, 4, 2, 2, 2
GROUP = NZ * NYL
BOTH = ("seq", "head")
CROSS_FIRST = 3
DIRECT = (0, 1, 6, 7)
FORWARDED = (4, 5, 2, 3)


def device_pairs(move):
    pairs = []
    for x in range(NX):
        for z in range(NZ):
            for y in range(NYL * NYH):
                for core in range(NCORE):
                    there = move(x, z, y, core)
                    pairs.append(tuple(
                        ((a * NZ + b) * NYL + c % NYL) * (NYH * NCORE) + (c // NYL) * NCORE + d
                        for a, b, c, d in ((x, z, y, core), there)
                    ))
    return pairs


def hop(value, move):
    return lax.ppermute(value, BOTH, device_pairs(move))


def rotated(place, turn, sign):
    z, y = place // NYL, place % NYL
    z = (z + sign * (turn // NYL) + NZ) % NZ
    y = (y + turn) % NYL
    return z * NYL + y


def turn_hop(value, turn, planes=0):
    dz, dy = turn // NYL, turn % NYL
    return hop(
        value,
        lambda x, z, y, c: (
            (x + planes) % NX,
            (z + dz) % NZ,
            (y // NYL) * NYL + (y + dy) % NYL,
            c,
        ),
    )


def split_kernel(place_ref, q_ref, k_ref, v_ref, *rest):
    outs, ahead = rest[:GROUP], rest[GROUP : GROUP + len(DIRECT)]
    q_buf, k_buf, v_buf, in_sems, out_sems = rest[GROUP + len(DIRECT) :]
    loads = []
    for n, (source, buf) in enumerate(((k_ref, k_buf), (v_ref, v_buf), (q_ref, q_buf))):
        copy = pltpu.make_async_copy(source, buf, in_sems.at[n])
        copy.start()
        loads.append(copy)
    copies = []
    for n, buf in enumerate((k_buf, v_buf, q_buf)):
        loads[n].wait()
        for turn in range(GROUP):
            columns = pl.ds(pl.multiple_of(place_ref[turn] * HD, HD), HD)
            targets = [outs[turn].at[n]]
            if turn in DIRECT and n < 2:
                targets.append(ahead[DIRECT.index(turn)].at[n])
            for again, target in enumerate(targets):
                copy = pltpu.make_async_copy(
                    buf.at[:, columns], target, out_sems.at[again, turn * 3 + n]
                )
                copy.start()
                copies.append(copy)
    for copy in copies:
        copy.wait()


def split_heads(targets, q, k, v):
    rows = q.shape[0]
    anywhere = pl.BlockSpec(memory_space=pl.ANY)
    out = pl.pallas_call(
        split_kernel,
        grid_spec=pltpu.PrefetchScalarGridSpec(
            num_scalar_prefetch=1,
            grid=(1,),
            in_specs=[anywhere] * 3,
            out_specs=[anywhere] * (GROUP + len(DIRECT)),
            scratch_shapes=[pltpu.VMEM(q.shape, q.dtype)] * 3
            + [pltpu.SemaphoreType.DMA((3,)), pltpu.SemaphoreType.DMA((2, 3 * GROUP))],
        ),
        out_shape=[jax.ShapeDtypeStruct((3, rows, HD), q.dtype)] * GROUP
        + [jax.ShapeDtypeStruct((2, rows, HD), q.dtype)] * len(DIRECT),
        name="split_heads",
    )(targets, q, k, v)
    return out[:GROUP], dict(zip(DIRECT, out[GROUP:]))


def join_kernel(source_ref, *rest):
    pieces, out, buf, sems, out_sem = rest[:GROUP], *rest[GROUP:]
    copies = []
    for turn in range(GROUP):
        columns = pl.ds(pl.multiple_of(source_ref[turn] * HD, HD), HD)
        copy = pltpu.make_async_copy(pieces[turn], buf.at[:, columns], sems.at[turn])
        copy.start()
        copies.append(copy)
    for copy in copies:
        copy.wait()
    copy = pltpu.make_async_copy(buf, out, out_sem)
    copy.start()
    copy.wait()


def join_heads(sources, pieces):
    rows = pieces[0].shape[0]
    anywhere = pl.BlockSpec(memory_space=pl.ANY)
    return pl.pallas_call(
        join_kernel,
        grid_spec=pltpu.PrefetchScalarGridSpec(
            num_scalar_prefetch=1,
            grid=(1,),
            in_specs=[anywhere] * GROUP,
            out_specs=anywhere,
            scratch_shapes=[
                pltpu.VMEM((rows, GROUP * HD), pieces[0].dtype),
                pltpu.SemaphoreType.DMA((GROUP,)),
                pltpu.SemaphoreType.DMA,
            ],
        ),
        out_shape=jax.ShapeDtypeStruct((rows, GROUP * HD), pieces[0].dtype),
        name="join_heads",
    )(sources, *pieces)


def self_kernel(rows, begins_ref, place_ref, *rest):
    own, past_kv, outs = (rest[n * GROUP : (n + 1) * GROUP] for n in range(3))
    (
        kbuf, vbuf, qbuf, obuf, top, total, accum, scores_a, scores_b, weights_a, weights_b,
        factor_a, factor_b, in_sems, out_sems,
    ) = rest[3 * GROUP :]
    span = GROUP * rows
    copies = []
    for turn in range(GROUP):
        slot = place_ref[GROUP + turn] * rows
        moves = []
        for pieces, base in ((past_kv, 0), (own, span)):
            to = pl.ds(pl.multiple_of(base + slot, rows), rows)
            moves += [(pieces[turn].at[0], kbuf.at[to]), (pieces[turn].at[1], vbuf.at[to])]
        moves.append((own[turn].at[2], qbuf.at[pl.ds(pl.multiple_of(slot, rows), rows)]))
        for n, (source, target) in enumerate(moves):
            copy = pltpu.make_async_copy(source, target, in_sems.at[turn * 5 + n])
            copy.start()
            copies.append(copy)
    for copy in copies:
        copy.wait()

    def begin_of(position):
        found = begins_ref[0]
        for d in range(1, 8):
            found = jnp.where(begins_ref[d] <= position, begins_ref[d], found)
        return found

    blocks = 2 * span // KEYS
    row_in = lax.broadcasted_iota(jnp.int32, (rows, 1), 0)
    col_in = lax.broadcasted_iota(jnp.int32, (rows, KEYS), 1)
    slots = ((scores_a, weights_a, factor_a), (scores_b, weights_b, factor_b))

    def chunk(c, carried):
        first = span + c * rows
        here = pl.ds(pl.multiple_of(c * rows, rows), rows)
        row = first + row_in
        row_begin = jnp.full((rows, 1), begins_ref[0], jnp.int32)
        for d in range(1, 8):
            row_begin = jnp.where(begins_ref[d] <= row, begins_ref[d], row_begin)
        low_block = jnp.maximum(begin_of(first), 0) // KEYS
        clear_block = (begin_of(first + rows - 1) + KEYS - 1) // KEYS
        diagonal = first // KEYS
        last_block = (first + rows - 1) // KEYS
        top[...] = jnp.full(top.shape, NEG_LARGE, jnp.float32)
        total[...] = jnp.zeros(total.shape, jnp.float32)
        accum[...] = jnp.zeros(accum.shape, jnp.float32)
        weights_b[...] = jnp.zeros(weights_b.shape, jnp.bfloat16)
        factor_b[...] = jnp.ones(factor_b.shape, jnp.float32)

        def rows_of(block):
            return pl.ds(pl.multiple_of(jnp.clip(block, 0, blocks - 1) * KEYS, KEYS), KEYS)

        def score(slot, block):
            slots[slot][0][...] = lax.dot_general(
                qbuf[here, :],
                kbuf[rows_of(block), :],
                (((1,), (1,)), ((), ())),
                preferred_element_type=jnp.float32,
            )

        def mix(slot, block):
            accum[...] = accum[...] * slots[slot][2][...] + jnp.dot(
                slots[slot][1][...], vbuf[rows_of(block), :], preferred_element_type=jnp.float32
            )

        def weigh(slot, block, masked):
            scores = slots[slot][0][...]
            if masked:
                col = block * KEYS + col_in
                scores = jnp.where((col >= row_begin) & (col <= row), scores, NEG_LARGE)
            old_top = top[...]
            new_top = jnp.maximum(old_top, jnp.max(scores, axis=1, keepdims=True))
            parts = [
                jnp.exp2((scores[:, n * HD : (n + 1) * HD] - new_top) * EXP2_SCALE)
                for n in range(KEYS // HD)
            ]
            slots[slot][1][...] = jnp.concatenate(
                [part.astype(jnp.bfloat16) for part in parts], axis=1
            )
            factor = jnp.exp2((old_top - new_top) * EXP2_SCALE)
            slots[slot][2][...] = factor
            total[...] = total[...] * factor + functools.reduce(jnp.add, parts)
            top[...] = new_top

        def step(slot, block, masked):
            score(1 - slot, block + 1)
            weigh(slot, block, masked)
            mix(1 - slot, block - 1)

        pairs = (last_block - low_block + 2) // 2

        def pair(n, carried):
            block = low_block + 2 * n
            masked = (block < clear_block) | (block + 1 >= diagonal)

            @pl.when(masked)
            def _():
                step(0, block, True)
                step(1, block + 1, True)

            @pl.when(jnp.logical_not(masked))
            def _():
                step(0, block, False)
                step(1, block + 1, False)

            return carried

        score(0, low_block)
        lax.fori_loop(0, pairs, pair, 0)
        mix(1, low_block + 2 * pairs - 1)
        whole = jnp.sum(total[...], axis=1, keepdims=True)
        obuf[here, :] = (accum[...] / whole).astype(jnp.bfloat16)
        return carried

    lax.fori_loop(0, GROUP, chunk, 0)
    copies = []
    for turn in range(GROUP):
        at = pl.ds(pl.multiple_of(place_ref[turn] * rows, rows), rows)
        copy = pltpu.make_async_copy(obuf.at[at], outs[turn], out_sems.at[turn])
        copy.start()
        copies.append(copy)
    for copy in copies:
        copy.wait()


def self_attention(begins, places, own, past_kv):
    rows = own[0].shape[1]
    span = rows * GROUP
    anywhere = pl.BlockSpec(memory_space=pl.ANY)
    return pl.pallas_call(
        functools.partial(self_kernel, rows),
        grid_spec=pltpu.PrefetchScalarGridSpec(
            num_scalar_prefetch=2,
            grid=(1,),
            in_specs=[anywhere] * (2 * GROUP),
            out_specs=[anywhere] * GROUP,
            scratch_shapes=[
                pltpu.VMEM((2 * span, HD), jnp.bfloat16),
                pltpu.VMEM((2 * span, HD), jnp.bfloat16),
                pltpu.VMEM((span, HD), jnp.bfloat16),
                pltpu.VMEM((span, HD), jnp.bfloat16),
                *[pltpu.VMEM((rows, HD), jnp.float32)] * 3,
                *[pltpu.VMEM((rows, KEYS), jnp.float32)] * 2,
                *[pltpu.VMEM((rows, KEYS), jnp.bfloat16)] * 2,
                *[pltpu.VMEM((rows, HD), jnp.float32)] * 2,
                pltpu.SemaphoreType.DMA((5 * GROUP,)),
                pltpu.SemaphoreType.DMA((GROUP,)),
            ],
        ),
        out_shape=[jax.ShapeDtypeStruct((rows, HD), jnp.bfloat16)] * GROUP,
        name="self_attention",
    )(begins, places, *own, *past_kv)


def cross_kernel(
    rows, width, place_ref, seen_ref, q_ref, lat_a, lat_b, wk_ref, wv_ref, gate_ref, *rest
):
    out_ref, keys, values, mask_ref = rest[-4:]
    images, count = NX * NZ, mask_ref.shape[1]

    @pl.when(pl.program_id(0) == 0)
    def _():
        plane, z_here = place_ref[2 * GROUP], place_ref[0] // NYL
        column = lax.broadcasted_iota(jnp.int32, (1, count), 1)
        piece = (column % (count // 2)) // (LAT // 2)
        for tile in range(rows // TILE):
            row = jnp.zeros((1, count), jnp.int32)
            for away in range(images):
                image = lax.rem(plane - away // NZ + NX, NX) * NZ + lax.rem(
                    z_here - away % NZ + NZ, NZ
                )
                row = jnp.where(piece == away, seen_ref[image, tile], row)
            mask_ref[tile : tile + 1, :] = row

    gate = jnp.tanh(gate_ref[...])
    heads = wk_ref.shape[1] // HD
    half = lat_a.shape[0]
    for n, lat in enumerate((lat_a, lat_b)):
        part = lat[:, :width]
        at = pl.ds(n * half, half)
        keys[at, :] = jnp.dot(
            part, wk_ref[...], preferred_element_type=jnp.float32
        ).astype(jnp.bfloat16)
        values[at, :] = jnp.dot(
            part, wv_ref[...], preferred_element_type=jnp.float32
        ).astype(jnp.bfloat16)
    for tile in range(rows // TILE):
        visible = mask_ref[tile : tile + 1, :] == 1
        any_seen = functools.reduce(
            jnp.logical_or, [seen_ref[image, tile] == 1 for image in range(images)]
        )
        seen = jnp.full((TILE, HD), jnp.where(any_seen, 1, 0), jnp.int32) > 0
        for head in range(heads):
            mine = slice(head * HD, (head + 1) * HD)
            scores = lax.dot_general(
                q_ref[tile * TILE : (tile + 1) * TILE, mine],
                keys[:, mine],
                (((1,), (1,)), ((), ())),
                preferred_element_type=jnp.float32,
            )
            scores = jnp.where(visible, scores, NEG_LARGE)
            row_top = jnp.max(scores, axis=1, keepdims=True)
            weights = jnp.exp2((scores - row_top) * EXP2_SCALE)
            row_total = jnp.sum(weights, axis=1, keepdims=True)
            mixed = jnp.dot(
                weights.astype(jnp.bfloat16), values[:, mine], preferred_element_type=jnp.float32
            )
            mixed = jnp.where(seen, mixed / row_total, 0.0) * gate[:, mine]
            out_ref[tile * TILE : (tile + 1) * TILE, mine] = mixed.astype(jnp.bfloat16)


def cross_attention(
    places, seen, q, lat_a, lat_b, w_flat, gate, begin, end, earlier=None
):
    rows, columns = q.shape
    width = w_flat.shape[0]
    step = 2 * HD
    steps = columns // step
    count = lat_a.shape[0] + lat_b.shape[0]
    return pl.pallas_call(
        functools.partial(cross_kernel, rows, width),
        grid_spec=pltpu.PrefetchScalarGridSpec(
            num_scalar_prefetch=2,
            grid=(end - begin,),
            in_specs=[
                pl.BlockSpec((rows, step), lambda i, p, s: (0, i + begin)),
                pl.BlockSpec(lat_a.shape, lambda i, p, s: (0, 0)),
                pl.BlockSpec(lat_b.shape, lambda i, p, s: (0, 0)),
                pl.BlockSpec((width, step), lambda i, p, s: (0, i + begin)),
                pl.BlockSpec((width, step), lambda i, p, s: (0, i + begin + steps)),
                pl.BlockSpec((1, step), lambda i, p, s: (0, i + begin)),
            ]
            + [pl.BlockSpec(memory_space=pl.ANY)] * (earlier is not None),
            out_specs=pl.BlockSpec((rows, step), lambda i, p, s: (0, i + begin)),
            scratch_shapes=[pltpu.VMEM((count, step), jnp.bfloat16)] * 2
            + [pltpu.VMEM((8, count), jnp.int32)],
        ),
        out_shape=jax.ShapeDtypeStruct((rows, columns), jnp.bfloat16),
        input_output_aliases={} if earlier is None else {8: 0},
        name="cross_attention",
    )(
        places, seen, q, lat_a, lat_b, w_flat, w_flat, gate,
        *(() if earlier is None else (earlier,)),
    )


def body(q_self, k_self, v_self, doc_ids, q_cross, latents, w_latent, visibility, cross_gate):
    rows, columns = q_self.shape
    width = latents.shape[1]
    position = lax.axis_index("seq")
    plane = position // GROUP
    place = position % GROUP
    turns = jnp.arange(GROUP, dtype=jnp.int32)
    targets = rotated(place, turns, 1)
    sources = rotated(place, turns, -1)
    places = jnp.concatenate([targets, sources, plane[None]]).astype(jnp.int32)

    below = jnp.sum(
        (doc_ids[None, :] < jnp.arange(8, dtype=jnp.int32)[:, None]).astype(jnp.int32), axis=1
    )
    lane = jnp.arange(HD, dtype=jnp.int32)[None, :]
    digits = jnp.where(lane == 0, (below // 16)[:, None], 0) + jnp.where(
        lane == 1, (below % 16)[:, None], 0
    )
    lat = jnp.concatenate([latents, digits.astype(jnp.bfloat16)], axis=1)
    pieces, ahead = split_heads(places, q_self, k_self, v_self)
    lat = jnp.concatenate(
        [lat] + [hop(lat, lambda x, z, y, c, d=d: (x, z, (y + d) % 4, c)) for d in (1, 2, 3)]
    )
    lat = jnp.concatenate(
        [lat] + [hop(lat, lambda x, z, y, c, d=d: (x, (z + d) % 4, y, c)) for d in (1, 2, 3)]
    )
    lat_a = jnp.concatenate(
        [lat] + [hop(lat, lambda x, z, y, c, d=d: ((x + d) % 4, z, y, c)) for d in (1, 2, 3)]
    )
    lat_b = hop(lat_a, lambda x, z, y, c: (x, z, y, 1 - c))

    counted = sum(
        jnp.sum(part[:, width : width + 2].astype(jnp.float32).reshape(-1, 8, 2), axis=0)
        for part in (lat_a, lat_b)
    ).astype(jnp.int32) // (NYH * NCORE)
    begins = counted[:, 0] * 16 + counted[:, 1] - (plane - 1) * GROUP * rows

    own = [pieces[0]] + [turn_hop(pieces[t], t) for t in range(1, GROUP)]
    passed = {t: own[t][:2] for t in FORWARDED}
    w_flat, passed[FORWARDED[0]] = lax.optimization_barrier(
        (w_latent.reshape(width, 2 * columns), passed[FORWARDED[0]])
    )
    past_kv = [
        turn_hop(ahead[t], t, 1)
        if t in DIRECT
        else hop(passed[t], lambda x, z, y, c: ((x + 1) % NX, z, y, c))
        for t in range(GROUP)
    ]
    gate = cross_gate.reshape(1, columns)
    operands = (places, visibility, q_cross, lat_a, lat_b, w_flat, gate)
    cross_mixed = cross_attention(*operands, 0, CROSS_FIRST)
    begins, cross_mixed = lax.optimization_barrier((begins, cross_mixed))
    mixed = self_attention(begins, places, own, past_kv)
    back = [mixed[0]] + [turn_hop(mixed[t], t) for t in range(1, GROUP)]
    self_mixed = join_heads(sources.astype(jnp.int32), back)
    cross_mixed = cross_attention(*operands, CROSS_FIRST, columns // (2 * HD), cross_mixed)
    return (cross_mixed, self_mixed)


def solution(mesh):
    placed = (
        P("seq", "head"),
        P("seq", "head"),
        P("seq", "head"),
        P("seq"),
        P("seq", "head"),
        P(("seq", "head"), None),
        P(None, None, "head"),
        P(None, "seq"),
        P("head"),
    )
    return jax.shard_map(
        body,
        mesh=mesh,
        in_specs=placed,
        out_specs=(P("seq", "head"), P("seq", "head")),
        check_vma=False,
    )
```
